128 devices in a mesh: dom: 128 (over x, y, z, core).
Axes of the slice: x: 4, y: 4, z: 4, core: 2. Of those that a mesh axis runs over, the one named last changes fastest.
Arguments:
- elevation: float32 [32768, 128], P('dom'), may hold values from -6 to 6
- momentum: float32 [32768, 2, 128], P('dom'), may hold values from -6 to 6
- depth: float32 [32768, 128], P('dom'), may hold values from 0.3 to 1.5
- drag: float32 [32768, 128], P('dom'), may hold values from 0.05 to 0.6
- div_weight: float32 [5, 2, 128, 128], replicated, may hold values from -0.078125 to 0.078125
- grad_weight: float32 [5, 128, 256], replicated, may hold values from -0.125 to 0.125
- neighbours: int32 [32768, 4], P('dom'), may hold values from 0 to 32767, as said below
- wet: int32 [4, 32768], P(None, 'dom'), may hold values from 0 to 1, as said below
- boundary_cells: int32 [32768], P('dom'), may hold values from 0 to 32767, as said below
- boundary_source: int32 [32768], P('dom'), may hold values from 0 to 16383
- series: float32 [4, 16384], P(None, 'dom'), may hold values from -6 to 6
- moved_from: int32 [32768], P('dom'), may hold values from 0 to 32767, as said below
Outputs:
- level_out: float32 [32768, 128], P('dom')
- flow_out: float32 [32768, 2, 128], P('dom')
The draws below stay inside these ranges and needn't reach their ends.
Inputs may be any that keep to these rules, and one draw needn't show every extreme that they name: Slots are left, right, lower, upper; the relation is mutual (b is c's right iff c is b's left, likewise lower and upper). Left and right neighbours lie on the block's own device; a lower neighbour lies on the block's own device or on the device of index one lower, an upper one on its own device or on the device of index one higher (wrapping around). No block has neighbours on both adjacent devices. Exactly 128 blocks of a device have a neighbour on the lower adjacent device, and exactly 128 on the upper one. 1 marks a block that is wet in that step. `boundary_cells`: block times 128 plus element, within the device that holds the entry; distinct within a device. `moved_from`: A permutation. The blocks that move from one device to one device (itself included) number at most 4, and some pair reaches that in every draw.
All inputs are finite; a program needn't handle non-finite values.
Results may differ from the reference program's by a relative error of at most 0.0001.
Values sent between devices are 32-bit elements; how exact they have to be, the bound alone decides.
No kernel may reach another device: no remote copies, remote signals or barrier semaphores. Data moves between devices by JAX's collectives and lax.ppermute only.
A program may use at most 64 MiB of HBM per device.

```python
import math
import jax
import jax.numpy as jnp
from jax import lax

E = 128
ROW_BLOCKS = 128
BLK_DEV = 256
STEPS = 4
BND_DEV = 256
NBLK = 32768
NPAR = 16384
NBND = 32768
N_DOM = 128


def draw_neighbours(key, part):
    base = jax.random.fold_in(key, 101)
    ndevices = NBLK // BLK_DEV
    keys = jax.random.split(base, ndevices)
    shuffled = jax.vmap(lambda single: jax.random.permutation(single, BLK_DEV))(keys).astype(jnp.int32)
    offsets = jnp.arange(ndevices, dtype=jnp.int32)[:, None] * BLK_DEV
    grid_ids = (shuffled + offsets).reshape(-1, ROW_BLOCKS)
    left = jnp.roll(grid_ids, 1, axis=1)
    right = jnp.roll(grid_ids, -1, axis=1)
    lower = jnp.roll(grid_ids, 1, axis=0)
    upper = jnp.roll(grid_ids, -1, axis=0)
    stacked = jnp.stack([left, right, lower, upper], axis=-1).reshape(-1, 4)
    return jnp.zeros((NBLK, 4), jnp.int32).at[grid_ids.reshape(-1)].set(stacked)


def draw_wet(key, part):
    base = jax.random.fold_in(key, 202)
    first, second = jax.random.split(base)
    ndevices = NBLK // BLK_DEV
    limits = jax.random.randint(first, (ndevices,), 250, 1001)
    draws = jax.random.randint(second, (STEPS, NBLK), 0, 1000)
    return (draws < jnp.repeat(limits, BLK_DEV)[None, :]).astype(jnp.int32)


def draw_boundary_cells(key, part):
    base = jax.random.fold_in(key, 303)
    first, second = jax.random.split(base)
    ndevices = NBLK // BLK_DEV
    keys = jax.random.split(first, ndevices)
    chosen = jax.vmap(lambda single: jax.random.permutation(single, BLK_DEV)[:BND_DEV])(keys).astype(jnp.int32)
    inside = jax.random.randint(second, (ndevices, BND_DEV), 0, E)
    return (chosen * E + inside).reshape(-1).astype(jnp.int32)


def draw_moved_from(key, part):
    base = jax.random.fold_in(key, 404)
    first, second = jax.random.split(base)
    ndevices = NBLK // BLK_DEV
    share = BLK_DEV // ndevices
    primary = jax.random.permutation(first, ndevices).astype(jnp.int32)
    missing = jnp.roll(primary, 1)
    targets = jnp.arange(ndevices, dtype=jnp.int32)
    counts = share * (1 + (targets[None, :] == primary[:, None]).astype(jnp.int32) - (targets[None, :] == missing[:, None]).astype(jnp.int32))
    column_sums = jnp.cumsum(counts, axis=0)
    row_starts = jnp.cumsum(counts, axis=1) - counts
    keys = jax.random.split(second, ndevices)
    shuffled = jax.vmap(lambda single: jax.random.permutation(single, BLK_DEV))(keys).astype(jnp.int32)
    slots = jnp.arange(NBLK, dtype=jnp.int32)
    target = slots // BLK_DEV
    within = slots % BLK_DEV
    source = jnp.sum((column_sums[:, target].T <= within[:, None]).astype(jnp.int32), axis=1)
    start = column_sums[source, target] - counts[source, target]
    offset = within - start
    local = shuffled[source, row_starts[source, target] + offset]
    return (source * BLK_DEV + local).astype(jnp.int32)


def set_ends(result, own_key, low, top_value):
    longest = result.shape.index(max(result.shape))
    spots = []
    for shift in (0, 1):
        where = [jax.random.randint(jax.random.fold_in(own_key, axis), (), 0, length) for axis, length in enumerate(result.shape)]
        where[longest] = (where[longest] + shift) % result.shape[longest]
        spots.append(tuple(where))
    return result.at[spots[0]].set(low).at[spots[1]].set(top_value)


def levels(stream_key, extent, cuts, smallest, high):
    factor_of = 1.0
    for axis_at, blocks in cuts:
        steps = jax.random.uniform(jax.random.fold_in(jax.random.fold_in(stream_key, 6), axis_at), (blocks,), jnp.float32, smallest / len(cuts), high / len(cuts))
        factor_of = factor_of * jnp.repeat(jnp.exp(steps), extent[axis_at] // blocks).reshape((-1,) + (1,) * (len(extent) - 1 - axis_at))
    return factor_of


def noise(stream_key, shape, width, bound, pieces=(), kind=jnp.bfloat16):
    result = jax.random.normal(stream_key, shape, jnp.float32) * width
    if len(pieces) > 0:
        result = levels(stream_key, shape, pieces, -0.22, 0.18) * result
    return jnp.clip(result, min=-bound, max=bound).astype(kind)


def setup_inputs(seed: int = 0) -> dict:
    arg_keys = jax.random.split(jax.random.key(seed), 13)
    return {
        "elevation": noise(arg_keys[0], (NBLK, E), 1.0, 6.0, ((0, 128),), jnp.float32),
        "momentum": noise(arg_keys[1], (NBLK, 2, E), 1.0, 6.0, ((0, 128),), jnp.float32),
        "depth": jnp.clip(jnp.exp(math.log(1.5) - 1.60943787 * jax.random.uniform(arg_keys[2], (NBLK, E), jnp.float32) ** levels(arg_keys[2], (NBLK, E), ((0, 128),), -0.2, 0.2)), 0.3, 1.5),
        "drag": jnp.clip(jnp.exp(math.log(0.6) - 2.4849067 * jax.random.uniform(arg_keys[3], (NBLK, E), jnp.float32) ** levels(arg_keys[3], (NBLK, E), ((0, 128),), -0.2, 0.2)), 0.05, 0.6),
        "div_weight": noise(arg_keys[4], (5, 2, E, E), (40 * E) ** -0.5, 0.078125, (), jnp.float32),
        "grad_weight": noise(arg_keys[5], (5, E, 2 * E), (20 * E) ** -0.5, 0.125, (), jnp.float32),
        "neighbours": draw_neighbours(jax.random.fold_in(arg_keys[12], 71), 0),
        "wet": draw_wet(jax.random.fold_in(arg_keys[12], 71), 0),
        "boundary_cells": draw_boundary_cells(jax.random.fold_in(arg_keys[12], 71), 0),
        "boundary_source": set_ends(jax.random.randint(arg_keys[9], (NBND,), 0, NPAR), jax.random.fold_in(arg_keys[9], 1), 0, NPAR - 1).astype(jnp.int32),
        "series": noise(arg_keys[10], (STEPS, NPAR), 1.0, 6.0, ((1, 128),), jnp.float32),
        "moved_from": draw_moved_from(jax.random.fold_in(arg_keys[12], 71), 0),
    }


relax_rate = 0.5
highest = lax.Precision.HIGHEST


def reference(elevation, momentum, depth, drag, div_weight, grad_weight, neighbours, wet, boundary_cells, boundary_source, series, moved_from):
    div_matrix = div_weight.reshape(10 * E, E)
    grad_matrix = grad_weight.reshape(5 * E, 2 * E)
    entry_device = jnp.arange(NBND, dtype=jnp.int32) // BND_DEV
    global_cells = (entry_device * (BLK_DEV * E) + boundary_cells).astype(jnp.int32)
    devices = jnp.arange(N_DOM, dtype=jnp.int32)
    for step in range(STEPS):
        mask = wet[step].astype(jnp.float32)[:, None]
        flows = momentum

        def divergence(device):
            rows = lax.dynamic_slice_in_dim(neighbours, device * BLK_DEV, BLK_DEV, 0)
            own = lax.dynamic_slice_in_dim(flows, device * BLK_DEV, BLK_DEV, 0)
            stacked = jnp.concatenate([own[:, None], flows[rows]], axis=1).reshape(BLK_DEV, 10 * E)
            return jnp.dot(stacked, div_matrix, precision=highest, preferred_element_type=jnp.float32)

        div = lax.map(divergence, devices).reshape(NBLK, E)
        level = elevation - mask * div
        flat = level.reshape(-1)
        forcing = series[step][boundary_source]
        flat = flat.at[global_cells].add(relax_rate * (forcing - flat[global_cells]))
        level = flat.reshape(NBLK, E)

        def gradient(device):
            rows = lax.dynamic_slice_in_dim(neighbours, device * BLK_DEV, BLK_DEV, 0)
            own = lax.dynamic_slice_in_dim(level, device * BLK_DEV, BLK_DEV, 0)
            stacked = jnp.concatenate([own[:, None], level[rows]], axis=1).reshape(BLK_DEV, 5 * E)
            return jnp.dot(stacked, grad_matrix, precision=highest, preferred_element_type=jnp.float32)

        grad = lax.map(gradient, devices).reshape(NBLK, 2, E)
        momentum = mask[:, :, None] * (momentum - depth[:, None] * grad) / (1.0 + drag)[:, None]
        elevation = level
    return elevation[moved_from], momentum[moved_from]
```

```python
import functools

import jax
import jax.numpy as jnp
from jax import lax
from jax.experimental import pallas as pl
from jax.experimental.pallas import tpu as pltpu
from jax.sharding import PartitionSpec as P

E = 128
HALF = 128
BLK = 256
STEPS = 4
SLOTS = 4
REQ = STEPS + 1
PAY = 2 * HALF
PAY_FIRST = PAY + 16

f32 = jnp.float32
bf16 = jnp.bfloat16
VMEM = pl.BlockSpec(memory_space=pltpu.VMEM)
SMEM = pl.BlockSpec(memory_space=pltpu.SMEM)


def dot(a, b):
    return lax.dot_general(a, b, (((1,), (0,)), ((), ())), preferred_element_type=f32)


def parts(x):
    hi = x.astype(bf16)
    return hi, (x - hi.astype(f32)).astype(bf16)


def wide(x):
    return jnp.concatenate(parts(x), axis=1)


def joined(x):
    n = x.shape[1] // 2
    return x[:, :n] + x[:, n:]


def pick(onehot, x):
    return joined(dot(onehot, wide(x)))


def ones(cond):
    return jnp.where(cond, 1.0, 0.0).astype(bf16)


def iota(shape, dim):
    return lax.broadcasted_iota(jnp.int32, shape, dim)


def row2(ref, at):
    return jnp.concatenate([ref[at : at + 1, :], ref[at + 1 : at + 2, :]], axis=1)


def ask_kernel(moved, series, operand, dest, rows):
    move_row = row2(moved, 0)
    rows[...] = jnp.zeros(rows.shape, f32)
    rows[0:1, :] = move_row.astype(f32)
    cols = jnp.transpose(rows[...])
    move_col = cols[:, 0:1].astype(jnp.int32)
    src_row, src_col = move_row >> 8, move_col >> 8
    lane = iota((BLK, BLK), 1)
    sub = iota((BLK, BLK), 0)
    earlier = jnp.where((src_row == src_col) & (lane < sub), 1.0, 0.0)
    rank = jnp.sum(earlier, axis=1, keepdims=True).astype(jnp.int32)
    lane1 = iota((BLK, HALF), 1)
    anchor = ((move_col & 255) + 1).astype(f32)
    placed = jnp.where(lane1 == rank, anchor, 0.0).astype(bf16)
    owners = ones(iota((HALF, BLK), 0) == src_row)
    wanted = dot(owners, placed) - 1.0
    for step in range(STEPS):
        operand[pl.ds(step, 128, stride=REQ), :] = jnp.broadcast_to(series[step : step + 1, :], (128, 128))
    operand[pl.ds(STEPS, 128, stride=REQ), :] = wanted
    for slot in range(SLOTS):
        dest[:, slot * 128 : (slot + 1) * 128] = ones((lane1 == src_col) & (rank == slot))


def diverge(step, m, elev, w_hi, w_lo, near, vert_e, vert_o, turn, keep, marks, part, q_e, q_o, pay_e, pay_o):
    hi, lo = parts(m)
    y = dot(hi, w_hi[...]) + dot(hi, w_lo[...]) + dot(lo, w_hi[...])
    acc = dot(near[0:BLK, :], wide(y[:, E : 2 * E])) + dot(near[BLK:, :], wide(y[:, 2 * E : 3 * E]))
    wide_e = wide(y[:, 3 * E : 4 * E])
    wide_o = wide(y[:, 4 * E : 5 * E])
    acc = acc + dot(vert_e[:, 0:BLK], wide_e) + dot(vert_o[:, 0:BLK], wide_o)
    div = y[:, 0:E] + joined(acc)
    mask = marks[:, step : step + 1]
    p = elev - mask * div
    part[...] = p
    to_e = joined(dot(turn[0:HALF, :], wide_o))
    to_o = joined(dot(turn[HALF:, :], wide_e))
    kept = pick(keep[...], p)
    q_e[...] = to_e
    q_o[...] = to_o
    pay_e[0:HALF, :] = to_e
    pay_o[0:HALF, :] = to_o
    pay_e[HALF : 2 * HALF, :] = kept[0:HALF, :]
    pay_o[HALF : 2 * HALF, :] = kept[HALF:, :]


def setup_kernel(
    parity, me, nb, drag, depth, elev, mom, dw, gw, wet, cells, points,
    pay_e, pay_o, part, q_e, q_o, m_out, w_hi, w_lo, g_hi, g_lo,
    near, vert_e, vert_o, turn, keep, back, marks, damp, dd, ids, rows,
):
    par = parity[0]
    even = par == 0
    own = me[0]
    slots = [0, 1, 2, 4 - par, 3 + par]
    for at, slot in enumerate(slots):
        hi, lo = parts(dw[slot])
        w_hi[:, at * E : (at + 1) * E] = hi
        w_lo[:, at * E : (at + 1) * E] = lo
        hi, lo = parts(gw[slot])
        g_hi[at * E : (at + 1) * E, :] = hi
        g_lo[at * E : (at + 1) * E, :] = lo
    lane = iota((BLK, BLK), 1)
    sub = iota((BLK, BLK), 0)
    lane1 = iota((BLK, HALF), 1)
    sub1 = iota((HALF, BLK), 0)
    left, right = nb[:, 0:1], nb[:, 1:2]
    low, up = nb[:, 2:3], nb[:, 3:4]
    nb_e = jnp.where(even, up, low)
    nb_o = jnp.where(even, low, up)
    id_e, id_o = nb_e & 255, nb_o & 255
    far_e, far_o = (nb_e >> 8) != own, (nb_o >> 8) != own
    near[0:BLK, :] = ones((left & 255) == lane)
    near[BLK:, :] = ones((right & 255) == lane)
    vert_e[:, 0:BLK] = ones((id_e == lane) & ~far_e)
    vert_o[:, 0:BLK] = ones((id_o == lane) & ~far_o)
    key_e = jnp.where(far_e, id_e, 512)
    key_o = jnp.where(far_o, id_o, 512)
    table = jnp.where(lane1 == 0, key_e, jnp.where(lane1 == 1, key_o, 0)).astype(f32)
    flat = jnp.transpose(table)
    key_e_row = flat[0:1, :].astype(jnp.int32)
    key_o_row = flat[1:2, :].astype(jnp.int32)
    for key, key_row, far, vert, at in (
        (key_e, key_e_row, far_e, vert_e, 0),
        (key_o, key_o_row, far_o, vert_o, HALF),
    ):
        far_row = key_row < 512
        rank = jnp.sum(jnp.where(key_row < key, 1.0, 0.0), axis=1, keepdims=True).astype(jnp.int32)
        vert[:, BLK:] = ones((rank == lane1) & far)
        rank_row = jnp.sum(jnp.where(key < key_row, 1.0, 0.0), axis=0, keepdims=True).astype(jnp.int32)
        turned = (rank_row == sub1) & far_row
        turn[at : at + HALF, :] = ones(turned)
        mine = jnp.sum(jnp.where((lane < sub) & far_row, 1.0, 0.0), axis=1, keepdims=True).astype(jnp.int32)
        back[:, at : at + HALF] = ones((mine == lane1) & far)
        mine_row = jnp.sum(jnp.where((sub < lane) & far, 1.0, 0.0), axis=0, keepdims=True).astype(jnp.int32)
        keep[at : at + HALF, :] = ones((mine_row == sub1) & far_row)
        partner = jnp.sum(jnp.where(turned, key_row, 0).astype(f32), axis=1, keepdims=True)
        ids[at : at + HALF, :] = jnp.broadcast_to(partner, (HALF, 128))
    rows[...] = jnp.zeros(rows.shape, f32)
    wet_f = wet[...].astype(f32)
    rows[0:STEPS, :] = wet_f
    marks[...] = jnp.transpose(rows[...])
    factor = 1.0 / (1.0 + drag[...])
    damp[...] = factor
    dd[...] = depth[...] * factor
    m = jnp.concatenate([mom[pl.ds(0, BLK, stride=2), :], mom[pl.ds(1, BLK, stride=2), :]], axis=1)
    m_out[...] = m
    diverge(0, m, elev[...], w_hi, w_lo, near, vert_e, vert_o, turn, keep, marks, part, q_e, q_o, pay_e, pay_o)
    tail = [wet_f[s : s + 1, h * 128 : (h + 1) * 128] for s in range(STEPS) for h in range(2)]
    cells_f, points_f = cells[...].astype(f32), points[...].astype(f32)
    tail = tail + [cells_f, points_f, jnp.zeros((4, 128), f32)]
    tail = jnp.concatenate(tail, axis=0)
    pay_e[PAY:, :] = tail
    pay_o[PAY:, :] = tail


def force_kernel(
    got, cells, points, in_e, in_o, ids, alpha, beta, alpha_e, beta_e, alpha_o, beta_o, marks_e, marks_o, rows
):
    tables = jnp.concatenate([got[pl.ds(s, 128, stride=REQ), :] for s in range(STEPS)], axis=1)
    tables = wide(tables)
    lists = [
        (row2(cells, 0), row2(points, 0)),
        (row2(in_e, PAY + 8).astype(jnp.int32), row2(in_e, PAY + 10).astype(jnp.int32)),
        (row2(in_o, PAY + 8).astype(jnp.int32), row2(in_o, PAY + 10).astype(jnp.int32)),
    ]
    rows[...] = jnp.zeros(rows.shape, f32)
    for at, (cell, point) in enumerate(lists):
        rows[2 * at : 2 * at + 1, :] = cell.astype(f32)
        rows[2 * at + 1 : 2 * at + 2, :] = point.astype(f32)
    cols = jnp.transpose(rows[...])
    lane1 = iota((BLK, 128), 1)
    sub = iota((BLK, BLK), 0)
    targets = [(alpha, beta), (alpha_e, beta_e), (alpha_o, beta_o)]
    for at, (cell_row, _) in enumerate(lists):
        cell = cols[:, 2 * at : 2 * at + 1].astype(jnp.int32)
        point = cols[:, 2 * at + 1 : 2 * at + 2].astype(jnp.int32)
        found = joined(dot(ones((point >> 7) == lane1), tables))
        spot = (point & 127) == lane1
        element = (cell & 127) == lane1
        values = []
        for step in range(STEPS):
            value = jnp.sum(jnp.where(spot, found[:, step * 128 : (step + 1) * 128], 0.0), axis=1, keepdims=True)
            values.append(jnp.where(element, 0.5 * value, 0.0))
        hi, lo = parts(jnp.concatenate(values, axis=1))
        half = jnp.where(element, 0.5, 0.0).astype(bf16)
        if at == 0:
            spread = ones(sub == (cell_row >> 7))
        else:
            key = ids[(at - 1) * HALF : at * HALF, 0:1].astype(jnp.int32)
            spread = ones(key == (cell_row >> 7))
        a_out, b_out = targets[at]
        a_out[...] = 1.0 - dot(spread, half)
        b_out[...] = dot(spread, hi) + dot(spread, lo)
    lane = iota((HALF, BLK), 1)
    for at, (in_ref, out) in enumerate(((in_e, marks_e), (in_o, marks_o))):
        here = ids[at * HALF : (at + 1) * HALF, 0:1].astype(jnp.int32) == lane
        total = jnp.zeros((HALF, 128), f32)
        lane0 = iota((HALF, 128), 1)
        for step in range(STEPS):
            flag = jnp.sum(jnp.where(here, row2(in_ref, PAY + 2 * step), 0.0), axis=1, keepdims=True)
            total = jnp.where(lane0 == step, flag, total)
        out[...] = total


def advance(
    step, in_e, in_o, part, q_e, q_o, m, g_hi, g_lo, near, vert_e, vert_o, back, marks, damp, dd,
    alpha, beta, alpha_e, beta_e, alpha_o, beta_o, marks_e, marks_o,
):
    at = slice(step * E, (step + 1) * E)
    mask = marks[:, step : step + 1]
    came = jnp.concatenate([in_e[0:HALF, :], in_o[0:HALF, :]], axis=0)
    level = alpha[...] * (part[...] - mask * pick(back[...], came)) + beta[:, at]
    edge_e = alpha_e[...] * (in_e[HALF:PAY, :] - marks_e[:, step : step + 1] * q_e[...]) + beta_e[:, at]
    edge_o = alpha_o[...] * (in_o[HALF:PAY, :] - marks_o[:, step : step + 1] * q_o[...]) + beta_o[:, at]
    both = wide(level)
    sides = dot(near[...], both).astype(bf16)
    up_e = (dot(vert_e[:, 0:BLK], both) + dot(vert_e[:, BLK:], wide(edge_e))).astype(bf16)
    up_o = (dot(vert_o[:, 0:BLK], both) + dot(vert_o[:, BLK:], wide(edge_o))).astype(bf16)
    pieces = [both, sides[0:BLK, :], sides[BLK:, :], up_e, up_o]
    hi = jnp.concatenate([p[:, 0:E] for p in pieces], axis=1)
    lo = jnp.concatenate([p[:, E:] for p in pieces], axis=1)
    grad = dot(hi, g_hi[...]) + dot(hi, g_lo[...]) + dot(lo, g_hi[...])
    d2 = jnp.concatenate([damp[...], damp[...]], axis=1)
    dd2 = jnp.concatenate([dd[...], dd[...]], axis=1)
    return level, mask * (d2 * m[...] - dd2 * grad)


def step_kernel(
    step, in_e, in_o, part, q_e, q_o, m, w_hi, w_lo, g_hi, g_lo, near, vert_e, vert_o, turn, keep, back, marks, damp,
    dd, alpha, beta, alpha_e, beta_e, alpha_o, beta_o, marks_e, marks_o,
    pay_e, pay_o, part_new, q_e_new, q_o_new, m_new,
):
    level, moved = advance(
        step, in_e, in_o, part, q_e, q_o, m, g_hi, g_lo, near, vert_e, vert_o, back, marks, damp, dd,
        alpha, beta, alpha_e, beta_e, alpha_o, beta_o, marks_e, marks_o,
    )
    m_new[...] = moved
    diverge(
        step + 1, moved, level, w_hi, w_lo, near, vert_e, vert_o, turn, keep, marks,
        part_new, q_e_new, q_o_new, pay_e, pay_o,
    )


def last_kernel(
    step, got, in_e, in_o, part, q_e, q_o, m, g_hi, g_lo, near, vert_e, vert_o, back, marks, damp,
    dd, alpha, beta, alpha_e, beta_e, alpha_o, beta_o, marks_e, marks_o, send,
):
    level, moved = advance(
        step, in_e, in_o, part, q_e, q_o, m, g_hi, g_lo, near, vert_e, vert_o, back, marks, damp, dd,
        alpha, beta, alpha_e, beta_e, alpha_o, beta_o, marks_e, marks_o,
    )
    state = wide(jnp.concatenate([level, moved], axis=1))
    wanted = got[pl.ds(STEPS, 128, stride=REQ), :].astype(jnp.int32)
    lane = iota((128, BLK), 1)
    for slot in range(SLOTS):
        chosen = joined(dot(ones(wanted[:, slot : slot + 1] == lane), state))
        for q in range(3):
            send[pl.ds(q * SLOTS + slot, 128, stride=3 * SLOTS), :] = chosen[:, q * 128 : (q + 1) * 128]


def place_kernel(back, dest, level_out, flow_out):
    state = []
    for slot in range(SLOTS):
        state.append(
            jnp.concatenate([back[pl.ds(q * SLOTS + slot, 128, stride=3 * SLOTS), :] for q in range(3)], axis=1)
        )
    out = pick(dest[...], jnp.concatenate(state, axis=0))
    level_out[...] = out[:, 0:E]
    flow_out[pl.ds(0, BLK, stride=2), :] = out[:, E : 2 * E]
    flow_out[pl.ds(1, BLK, stride=2), :] = out[:, 2 * E :]


def shape(*dims, dtype=f32):
    return jax.ShapeDtypeStruct(dims, dtype)


def call(kernel, outs, args, name, flops, smem=0, scratch=()):
    moved = sum(a.size * a.dtype.itemsize for a in args)
    return pl.pallas_call(
        kernel,
        out_shape=tuple(outs),
        in_specs=[SMEM] * smem + [VMEM] * (len(args) - smem),
        out_specs=tuple(VMEM for _ in outs),
        scratch_shapes=list(scratch),
        cost_estimate=pl.CostEstimate(flops=flops, bytes_accessed=moved, transcendentals=0),
        name=name,
    )(*args)


def local(
    elevation, momentum, depth, drag, div_weight, grad_weight, neighbours, wet,
    boundary_cells, boundary_source, series, moved_from,
):
    count = lax.axis_size("dom")
    device = lax.axis_index("dom")
    inside = [(i, i ^ 1) for i in range(count)]
    between = [((2 * i + 1) % count, (2 * i + 2) % count) for i in range(count // 2)]
    between = between + [(b, a) for a, b in between]
    parity = (device % 2).astype(jnp.int32).reshape(1)
    me = device.astype(jnp.int32).reshape(1)
    cells = boundary_cells.reshape(2, 128)
    points = boundary_source.reshape(2, 128)
    line = pltpu.VMEM((128, BLK), f32)

    operand, dest = call(
        ask_kernel,
        [shape(count * REQ, 128), shape(BLK, SLOTS * 128, dtype=bf16)],
        [moved_from.reshape(2, 128), series],
        "ask", 10**7, scratch=[line],
    )
    got = lax.all_to_all(operand.reshape(count, 1, REQ * 128), "dom", split_axis=0, concat_axis=0, tiled=True)
    got = got.reshape(count * REQ, 128)

    (pay_e, pay_o, part, q_e, q_o, m, w_hi, w_lo, g_hi, g_lo, near, vert_e, vert_o, turn, keep, back, marks, damp,
     dd, ids) = call(
        setup_kernel,
        [
            shape(PAY_FIRST, 128), shape(PAY_FIRST, 128), shape(BLK, E), shape(HALF, E), shape(HALF, E),
            shape(BLK, 2 * E), shape(2 * E, 5 * E, dtype=bf16), shape(2 * E, 5 * E, dtype=bf16),
            shape(5 * E, 2 * E, dtype=bf16), shape(5 * E, 2 * E, dtype=bf16),
            shape(2 * BLK, BLK, dtype=bf16), shape(BLK, BLK + HALF, dtype=bf16), shape(BLK, BLK + HALF, dtype=bf16),
            shape(BLK, BLK, dtype=bf16), shape(BLK, BLK, dtype=bf16), shape(BLK, BLK, dtype=bf16),
            shape(BLK, 128), shape(BLK, E), shape(BLK, E), shape(BLK, 128),
        ],
        [
            parity, me, neighbours, drag, depth, elevation, momentum.reshape(2 * BLK, E),
            div_weight.reshape(5, 2 * E, E), grad_weight, wet, cells, points,
        ],
        "setup", 10**9, smem=2, scratch=[line],
    )
    tables = [g_hi, g_lo, near, vert_e, vert_o]
    more = [back, marks, damp, dd]
    forcing = None
    for step in range(STEPS):
        in_e = lax.ppermute(pay_e, "dom", inside)
        in_o = lax.ppermute(pay_o, "dom", between)
        if forcing is None:
            forcing = list(call(
                force_kernel,
                [
                    shape(BLK, E), shape(BLK, STEPS * E), shape(HALF, E), shape(HALF, STEPS * E),
                    shape(HALF, E), shape(HALF, STEPS * E), shape(HALF, 128), shape(HALF, 128),
                ],
                [got, cells, points, in_e, in_o, ids],
                "force", 10**9, scratch=[line],
            ))
        if step < STEPS - 1:
            pay_e, pay_o, part, q_e, q_o, m = call(
                functools.partial(step_kernel, step),
                [
                    shape(PAY, 128), shape(PAY, 128), shape(BLK, E), shape(HALF, E), shape(HALF, E), shape(BLK, 2 * E),
                ],
                [in_e, in_o, part, q_e, q_o, m, w_hi, w_lo] + tables + [turn, keep] + more + forcing,
                "step", 10**9,
            )
        else:
            (send,) = call(
                functools.partial(last_kernel, step),
                [shape(count * 3 * SLOTS, 128)],
                [got, in_e, in_o, part, q_e, q_o, m] + tables + more + forcing,
                "last", 10**9,
            )
    returned = lax.all_to_all(send.reshape(count, 1, 3 * SLOTS * 128), "dom", split_axis=0, concat_axis=0, tiled=True)
    level_out, flow_out = call(
        place_kernel,
        [shape(BLK, E), shape(2 * BLK, E)],
        [returned.reshape(count * 3 * SLOTS, 128), dest],
        "place", 10**9,
    )
    return level_out, flow_out.reshape(BLK, 2, E)


def solution(mesh):
    return jax.shard_map(
        local,
        mesh=mesh,
        in_specs=(
            P("dom", None),
            P("dom", None, None),
            P("dom", None),
            P("dom", None),
            P(),
            P(),
            P("dom", None),
            P(None, "dom"),
            P("dom"),
            P("dom"),
            P(None, "dom"),
            P("dom"),
        ),
        out_specs=(P("dom", None), P("dom", None, None)),
        check_vma=False,
    )
```

```python
import functools

import jax
import jax.numpy as jnp
from jax import lax
from jax.experimental import pallas as pl
from jax.experimental.pallas import tpu as pltpu
from jax.sharding import PartitionSpec as P


E = 128
HALF = 128
BLK = 256
STEPS = 4
SLOTS = 4
REQ = STEPS + 1
WET = 4
IDS = 16
MINE = 17
SRC = 19
RANK = 20
PAY = 2 * HALF
PAY_FIRST = PAY + 16

f32 = jnp.float32
bf16 = jnp.bfloat16
VMEM = pl.BlockSpec(memory_space=pltpu.VMEM)
SMEM = pl.BlockSpec(memory_space=pltpu.SMEM)


def dot(a, b):
    return lax.dot_general(a, b, (((1,), (0,)), ((), ())), preferred_element_type=f32)


def parts(x):
    hi = x.astype(bf16)
    return hi, (x - hi.astype(f32)).astype(bf16)


def wide(x):
    return jnp.concatenate(parts(x), axis=1)


def joined(x):
    n = x.shape[1] // 2
    return x[:, :n] + x[:, n:]


def pick(onehot, x):
    return joined(dot(onehot, wide(x)))


def ones(cond):
    return jnp.where(cond, 1.0, 0.0).astype(bf16)


def iota(shape, dim):
    return lax.broadcasted_iota(jnp.int32, shape, dim)


def row2(ref, at):
    return jnp.concatenate([ref[at : at + 1, :], ref[at + 1 : at + 2, :]], axis=1)


def diverge(step, m, elev, w_hi, w_lo, near, vert_e, vert_o, turn, keep, marks, loc, pay_e, pay_o):
    hi, lo = parts(m)
    y = dot(hi, w_hi[...]) + dot(hi, w_lo[...]) + dot(lo, w_hi[...])
    acc = dot(near[0:BLK, :], wide(y[:, E : 2 * E])) + dot(near[BLK:, :], wide(y[:, 2 * E : 3 * E]))
    wide_e = wide(y[:, 3 * E : 4 * E])
    wide_o = wide(y[:, 4 * E : 5 * E])
    acc = acc + dot(vert_e[:, 0:BLK], wide_e) + dot(vert_o[:, 0:BLK], wide_o)
    div = y[:, 0:E] + joined(acc)
    mask = marks[:, WET + step : WET + step + 1]
    p = elev - mask * div
    loc[0:BLK, :] = p
    to_e = joined(dot(turn[0:HALF, :], wide_o))
    to_o = joined(dot(turn[HALF:, :], wide_e))
    kept = pick(keep[...], p)
    loc[BLK : BLK + HALF, :] = to_e
    loc[BLK + HALF :, :] = to_o
    pay_e[0:HALF, :] = to_e
    pay_o[0:HALF, :] = to_o
    pay_e[HALF : 2 * HALF, :] = kept[0:HALF, :]
    pay_o[HALF : 2 * HALF, :] = kept[HALF:, :]


def setup_kernel(
    parity, me, moved_h, series_h, nb_h, wet_h, cells_h, points_h, mom_h, dw_h, elev_h,
    operand, pay_e, pay_o, loc, m_out, w_hi, w_lo, near, vert_e, vert_o, turn, keep, marks,
    moved, series, nb, wet, cells, points, mom, dw, elev, rows, sems,
):
    pairs = [
        (moved_h, moved), (nb_h, nb), (wet_h, wet), (series_h, series), (cells_h, cells), (points_h, points),
        (mom_h, mom), (dw_h, dw), (elev_h, elev),
    ]
    copies = [pltpu.make_async_copy(src, dst, sems.at[i]) for i, (src, dst) in enumerate(pairs)]
    for copy in copies:
        copy.start()
    par = parity[0]
    even = par == 0
    own = me[0]
    lane = iota((BLK, BLK), 1)
    sub = iota((BLK, BLK), 0)
    lane1 = iota((BLK, HALF), 1)
    sub1 = iota((HALF, BLK), 0)
    rows[...] = jnp.zeros(rows.shape, f32)
    for copy in copies[:6]:
        copy.wait()
    move_row = row2(moved, 0)
    wet_f = wet[...].astype(f32)
    rows[0:4, :] = nb[...].astype(f32)
    rows[4:8, :] = wet_f
    rows[8:9, :] = move_row.astype(f32)
    cols = jnp.transpose(rows[...])

    move_col = cols[:, 8:9].astype(jnp.int32)
    src_row, src_col = move_row >> 8, move_col >> 8
    earlier = jnp.where((src_row == src_col) & (lane < sub), 1.0, 0.0)
    rank = jnp.sum(earlier, axis=1, keepdims=True).astype(jnp.int32)
    anchor = ((move_col & 255) + 1).astype(f32)
    placed = jnp.where(lane1 == rank, anchor, 0.0).astype(bf16)
    wanted = dot(ones(sub1 == src_row), placed) - 1.0
    for step in range(STEPS):
        operand[pl.ds(step, 128, stride=REQ), :] = jnp.broadcast_to(series[step : step + 1, :], (128, 128))
    operand[pl.ds(STEPS, 128, stride=REQ), :] = wanted
    notes = jnp.where(lane1 == SRC, src_col, jnp.where(lane1 == RANK, rank, 0)).astype(f32)

    ints = cols[:, 0:8].astype(jnp.int32)
    left, right, low, up = (ints[:, k : k + 1] for k in range(4))
    low_row, up_row = nb[2:3, :], nb[3:4, :]
    near[0:BLK, :] = ones((left & 255) == lane)
    near[BLK:, :] = ones((right & 255) == lane)
    partners = []
    for nb_col, nb_row, vert, at in (
        (jnp.where(even, up, low), jnp.where(even, up_row, low_row), vert_e, 0),
        (jnp.where(even, low, up), jnp.where(even, low_row, up_row), vert_o, HALF),
    ):
        far, far_row = (nb_col >> 8) != own, (nb_row >> 8) != own
        local_col, local_row = nb_col & 255, nb_row & 255
        vert[:, 0:BLK] = ones((local_col == lane) & ~far)
        key, key_row = jnp.where(far, local_col, 512), jnp.where(far_row, local_row, 512)
        rank = jnp.sum(jnp.where(key_row < key, 1.0, 0.0), axis=1, keepdims=True).astype(jnp.int32)
        vert[:, BLK:] = ones((rank == lane1) & far)
        rank_row = jnp.sum(jnp.where(key < key_row, 1.0, 0.0), axis=0, keepdims=True).astype(jnp.int32)
        turned = (rank_row == sub1) & far_row
        turn[at : at + HALF, :] = ones(turned)
        mine = jnp.sum(jnp.where((lane < sub) & far_row, 1.0, 0.0), axis=1, keepdims=True).astype(jnp.int32)
        notes = jnp.where(lane1 == MINE + at // HALF, jnp.where(far, mine, 512).astype(f32), notes)
        mine_row = jnp.sum(jnp.where((sub < lane) & far, 1.0, 0.0), axis=0, keepdims=True).astype(jnp.int32)
        keep[at : at + HALF, :] = ones((mine_row == sub1) & far_row)
        partners.append(jnp.sum(jnp.where(turned, key_row, 0).astype(f32), axis=1, keepdims=True))
    notes = jnp.where(lane1 == IDS, jnp.concatenate(partners, axis=0), notes)
    marks[...] = jnp.where(lane1 < 16, cols, notes)

    slots = [0, 1, 2, 4 - par, 3 + par]
    copies[6].wait()
    copies[7].wait()
    for at, slot in enumerate(slots):
        hi, lo = parts(dw[slot])
        w_hi[:, at * E : (at + 1) * E] = hi
        w_lo[:, at * E : (at + 1) * E] = lo
    m = jnp.concatenate([mom[pl.ds(0, BLK, stride=2), :], mom[pl.ds(1, BLK, stride=2), :]], axis=1)
    m_out[...] = m
    copies[8].wait()
    diverge(0, m, elev[...], w_hi, w_lo, near, vert_e, vert_o, turn, keep, marks, loc, pay_e, pay_o)
    tail = [wet_f[s : s + 1, h * 128 : (h + 1) * 128] for s in range(STEPS) for h in range(2)]
    cells_f, points_f = cells[...].astype(f32), points[...].astype(f32)
    tail = jnp.concatenate(tail + [cells_f, points_f, jnp.zeros((4, 128), f32)], axis=0)
    pay_e[PAY:, :] = tail
    pay_o[PAY:, :] = tail


def force_kernel(
    parity, got, in_e, in_o, marks, cells_h, points_h, gw_h, drag_h, depth_h,
    g_hi, g_lo, back, damp, dd, alpha, beta, alpha_e, beta_e, alpha_o, beta_o, marks_e, marks_o,
    cells, points, gw, drag, depth, rows, sems,
):
    pairs = [(cells_h, cells), (points_h, points), (gw_h, gw), (drag_h, drag), (depth_h, depth)]
    copies = [pltpu.make_async_copy(src, dst, sems.at[i]) for i, (src, dst) in enumerate(pairs)]
    for copy in copies:
        copy.start()
    par = parity[0]
    tables = jnp.concatenate([got[pl.ds(s, 128, stride=REQ), :] for s in range(STEPS)], axis=1)
    tables = wide(tables)
    copies[0].wait()
    copies[1].wait()
    lists = [
        (row2(cells, 0), row2(points, 0)),
        (row2(in_e, PAY + 8).astype(jnp.int32), row2(in_e, PAY + 10).astype(jnp.int32)),
        (row2(in_o, PAY + 8).astype(jnp.int32), row2(in_o, PAY + 10).astype(jnp.int32)),
    ]
    rows[...] = jnp.zeros(rows.shape, f32)
    for at, (cell, point) in enumerate(lists):
        rows[2 * at : 2 * at + 1, :] = cell.astype(f32)
        rows[2 * at + 1 : 2 * at + 2, :] = point.astype(f32)
    cols = jnp.transpose(rows[...])
    lane1 = iota((BLK, 128), 1)
    sub = iota((BLK, BLK), 0)
    targets = [(alpha, beta), (alpha_e, beta_e), (alpha_o, beta_o)]
    for at, (cell_row, _) in enumerate(lists):
        cell = cols[:, 2 * at : 2 * at + 1].astype(jnp.int32)
        point = cols[:, 2 * at + 1 : 2 * at + 2].astype(jnp.int32)
        found = joined(dot(ones((point >> 7) == lane1), tables))
        spot = (point & 127) == lane1
        element = (cell & 127) == lane1
        values = []
        for step in range(STEPS):
            value = jnp.sum(jnp.where(spot, found[:, step * 128 : (step + 1) * 128], 0.0), axis=1, keepdims=True)
            values.append(jnp.where(element, 0.5 * value, 0.0))
        hi, lo = parts(jnp.concatenate(values, axis=1))
        half = jnp.where(element, 0.5, 0.0).astype(bf16)
        if at == 0:
            spread = ones(sub == (cell_row >> 7))
        else:
            key = marks[(at - 1) * HALF : at * HALF, IDS : IDS + 1].astype(jnp.int32)
            spread = ones(key == (cell_row >> 7))
        a_out, b_out = targets[at]
        a_out[...] = 1.0 - dot(spread, half)
        b_out[...] = dot(spread, hi) + dot(spread, lo)
    lane = iota((HALF, BLK), 1)
    for at, (in_ref, out) in enumerate(((in_e, marks_e), (in_o, marks_o))):
        here = marks[at * HALF : (at + 1) * HALF, IDS : IDS + 1].astype(jnp.int32) == lane
        total = jnp.zeros((HALF, 128), f32)
        lane0 = iota((HALF, 128), 1)
        for step in range(STEPS):
            flag = jnp.sum(jnp.where(here, row2(in_ref, PAY + 2 * step), 0.0), axis=1, keepdims=True)
            total = jnp.where(lane0 == step, flag, total)
        out[...] = total
    for at in range(2):
        mine = marks[:, MINE + at : MINE + at + 1].astype(jnp.int32)
        back[:, at * HALF : (at + 1) * HALF] = ones(mine == lane1)
    for copy in copies[2:]:
        copy.wait()
    for at, slot in enumerate([0, 1, 2, 4 - par, 3 + par]):
        hi, lo = parts(gw[slot])
        g_hi[at * E : (at + 1) * E, :] = hi
        g_lo[at * E : (at + 1) * E, :] = lo
    factor = 1.0 / (1.0 + drag[...])
    damp[...] = factor
    dd[...] = depth[...] * factor


def advance(
    step, in_e, in_o, loc, m, g_hi, g_lo, near, vert_e, vert_o, back, marks, damp, dd,
    alpha, beta, alpha_e, beta_e, alpha_o, beta_o, marks_e, marks_o,
):
    at = slice(step * E, (step + 1) * E)
    mask = marks[:, WET + step : WET + step + 1]
    came = jnp.concatenate([in_e[0:HALF, :], in_o[0:HALF, :]], axis=0)
    level = alpha[...] * (loc[0:BLK, :] - mask * pick(back[...], came)) + beta[:, at]
    edge_e = alpha_e[...] * (in_e[HALF:PAY, :] - marks_e[:, step : step + 1] * loc[BLK : BLK + HALF, :]) + beta_e[:, at]
    edge_o = alpha_o[...] * (in_o[HALF:PAY, :] - marks_o[:, step : step + 1] * loc[BLK + HALF :, :]) + beta_o[:, at]
    both = wide(level)
    sides = dot(near[...], both).astype(bf16)
    up_e = (dot(vert_e[:, 0:BLK], both) + dot(vert_e[:, BLK:], wide(edge_e))).astype(bf16)
    up_o = (dot(vert_o[:, 0:BLK], both) + dot(vert_o[:, BLK:], wide(edge_o))).astype(bf16)
    pieces = [both, sides[0:BLK, :], sides[BLK:, :], up_e, up_o]
    hi = jnp.concatenate([p[:, 0:E] for p in pieces], axis=1)
    lo = jnp.concatenate([p[:, E:] for p in pieces], axis=1)
    grad = dot(hi, g_hi[...]) + dot(hi, g_lo[...]) + dot(lo, g_hi[...])
    d2 = jnp.concatenate([damp[...], damp[...]], axis=1)
    dd2 = jnp.concatenate([dd[...], dd[...]], axis=1)
    return level, mask * (d2 * m[...] - dd2 * grad)


def step_kernel(
    step, in_e, in_o, loc, m, w_hi, w_lo, near, vert_e, vert_o, turn, keep, marks, g_hi, g_lo, back, damp,
    dd, alpha, beta, alpha_e, beta_e, alpha_o, beta_o, marks_e, marks_o,
    pay_e, pay_o, loc_new, m_new,
):
    level, moved = advance(
        step, in_e, in_o, loc, m, g_hi, g_lo, near, vert_e, vert_o, back, marks, damp, dd,
        alpha, beta, alpha_e, beta_e, alpha_o, beta_o, marks_e, marks_o,
    )
    m_new[...] = moved
    diverge(
        step + 1, moved, level, w_hi, w_lo, near, vert_e, vert_o, turn, keep, marks,
        loc_new, pay_e, pay_o,
    )


def last_kernel(
    step, got, in_e, in_o, loc, m, near, vert_e, vert_o, marks, g_hi, g_lo, back, damp,
    dd, alpha, beta, alpha_e, beta_e, alpha_o, beta_o, marks_e, marks_o, send,
):
    level, moved = advance(
        step, in_e, in_o, loc, m, g_hi, g_lo, near, vert_e, vert_o, back, marks, damp, dd,
        alpha, beta, alpha_e, beta_e, alpha_o, beta_o, marks_e, marks_o,
    )
    state = wide(jnp.concatenate([level, moved], axis=1))
    wanted = got[pl.ds(STEPS, 128, stride=REQ), :].astype(jnp.int32)
    lane = iota((128, BLK), 1)
    for slot in range(SLOTS):
        chosen = joined(dot(ones(wanted[:, slot : slot + 1] == lane), state))
        for q in range(3):
            send[pl.ds(q * SLOTS + slot, 128, stride=3 * SLOTS), :] = chosen[:, q * 128 : (q + 1) * 128]


def place_kernel(returned, marks, level_out, flow_out):
    lane1 = iota((BLK, 128), 1)
    src = marks[:, SRC : SRC + 1].astype(jnp.int32)
    rank = marks[:, RANK : RANK + 1].astype(jnp.int32)
    dest = jnp.concatenate([ones((lane1 == src) & (rank == slot)) for slot in range(SLOTS)], axis=1)
    state = []
    for slot in range(SLOTS):
        state.append(
            jnp.concatenate([returned[pl.ds(q * SLOTS + slot, 128, stride=3 * SLOTS), :] for q in range(3)], axis=1)
        )
    out = pick(dest, jnp.concatenate(state, axis=0))
    level_out[...] = out[:, 0:E]
    flow_out[pl.ds(0, BLK, stride=2), :] = out[:, E : 2 * E]
    flow_out[pl.ds(1, BLK, stride=2), :] = out[:, 2 * E :]


def shape(*dims, dtype=f32):
    return pltpu.VMEM(dims, dtype)


def result(*dims):
    return jax.ShapeDtypeStruct(dims, f32)


def call(kernel, outs, args, flops, scratch=(), specs=None):
    moved = sum(a.size * a.dtype.itemsize for a in args)
    if specs is None:
        args = [pltpu.with_memory_space_constraint(a, pltpu.VMEM) for a in args]
    return pl.pallas_call(
        kernel,
        out_shape=tuple(outs),
        in_specs=specs or [VMEM] * len(args),
        out_specs=tuple(VMEM for _ in outs),
        scratch_shapes=list(scratch),
        compiler_params=pltpu.CompilerParams(vmem_limit_bytes=16 << 20),
        cost_estimate=pl.CostEstimate(flops=flops, bytes_accessed=moved, transcendentals=0),
    )(*args)


def local(
    elevation, momentum, depth, drag, div_weight, grad_weight, neighbours, wet,
    boundary_cells, boundary_source, series, moved_from,
):
    count = lax.axis_size("dom")
    device = lax.axis_index("dom")
    inside = [(i, i ^ 1) for i in range(count)]
    between = [((2 * i + 1) % count, (2 * i + 2) % count) for i in range(count // 2)]
    between = between + [(b, a) for a, b in between]
    parity = (device % 2).astype(jnp.int32).reshape(1)
    me = device.astype(jnp.int32).reshape(1)
    cells = boundary_cells.reshape(2, 128)
    points = boundary_source.reshape(2, 128)
    line = pltpu.VMEM((128, BLK), f32)

    def hbm(args):
        return [pltpu.with_memory_space_constraint(a, pltpu.HBM) for a in args]

    def scratch(args):
        return [pltpu.VMEM(a.shape, a.dtype) for a in args] + [line, pltpu.SemaphoreType.DMA((len(args),))]

    anywhere = pl.BlockSpec(memory_space=pl.ANY)
    raw = [
        moved_from.reshape(2, 128), series, neighbours.T, wet, cells, points, momentum.reshape(2 * BLK, E),
        div_weight.reshape(5, 2 * E, E), elevation,
    ]
    later = [cells, points, grad_weight, drag, depth]
    (operand, pay_e, pay_o, loc, m, w_hi, w_lo, near, vert_e, vert_o, turn, keep, marks) = call(
        setup_kernel,
        [
            result(count * REQ, 128),
            shape(PAY_FIRST, 128), shape(PAY_FIRST, 128), shape(2 * BLK, E),
            shape(BLK, 2 * E), shape(2 * E, 5 * E, dtype=bf16), shape(2 * E, 5 * E, dtype=bf16),
            shape(2 * BLK, BLK, dtype=bf16), shape(BLK, BLK + HALF, dtype=bf16), shape(BLK, BLK + HALF, dtype=bf16),
            shape(BLK, BLK, dtype=bf16), shape(BLK, BLK, dtype=bf16), shape(BLK, 128),
        ],
        [parity, me] + hbm(raw),
        10**9, scratch=scratch(raw), specs=[SMEM] * 2 + [anywhere] * len(raw),
    )
    forcing = None
    for step in range(STEPS):
        in_e = lax.ppermute(pay_e, "dom", inside)
        in_o = lax.ppermute(pay_o, "dom", between)
        if forcing is None:
            got = lax.all_to_all(operand.reshape(count, 1, REQ * 128), "dom", split_axis=0, concat_axis=0, tiled=True)
        if forcing is None:
            got = got.reshape(count * REQ, 128)
            near_args = [pltpu.with_memory_space_constraint(a, pltpu.VMEM) for a in (got, in_e, in_o, marks)]
            forcing = list(call(
                force_kernel,
                [
                    shape(5 * E, 2 * E, dtype=bf16), shape(5 * E, 2 * E, dtype=bf16), shape(BLK, BLK, dtype=bf16),
                    shape(BLK, E), shape(BLK, E),
                    shape(BLK, E), shape(BLK, STEPS * E), shape(HALF, E), shape(HALF, STEPS * E),
                    shape(HALF, E), shape(HALF, STEPS * E), shape(HALF, 128), shape(HALF, 128),
                ],
                [parity] + near_args + hbm(later),
                10**9, scratch=scratch(later), specs=[SMEM] + [VMEM] * 4 + [anywhere] * len(later),
            ))
        if step < STEPS - 1:
            pay_e, pay_o, loc, m = call(
                functools.partial(step_kernel, step),
                [shape(PAY, 128), shape(PAY, 128), shape(2 * BLK, E), shape(BLK, 2 * E)],
                [in_e, in_o, loc, m, w_hi, w_lo, near, vert_e, vert_o, turn, keep, marks] + forcing,
                10**9,
            )
        else:
            (send,) = call(
                functools.partial(last_kernel, step),
                [shape(count * 3 * SLOTS, 128)],
                [got, in_e, in_o, loc, m, near, vert_e, vert_o, marks] + forcing,
                10**9,
            )
    returned = lax.all_to_all(send.reshape(count, 1, 3 * SLOTS * 128), "dom", split_axis=0, concat_axis=0, tiled=True)
    level_out, flow_out = call(
        place_kernel, [result(BLK, E), result(2 * BLK, E)], [returned.reshape(count * 3 * SLOTS, 128), marks], 10**9
    )
    return level_out, flow_out.reshape(BLK, 2, E)


def solution(mesh):
    return jax.shard_map(
        local,
        mesh=mesh,
        in_specs=(
            P("dom", None),
            P("dom", None, None),
            P("dom", None),
            P("dom", None),
            P(),
            P(),
            P("dom", None),
            P(None, "dom"),
            P("dom"),
            P("dom"),
            P(None, "dom"),
            P("dom"),
        ),
        out_specs=(P("dom", None), P("dom", None, None)),
        check_vma=False,
    )
```
